256 devices in a mesh: grp: 4 (over y), seq: 64 (over x, z, core).
Axes of the slice: x: 4, y: 4, z: 8, core: 2. Of those that a mesh axis runs over, the one named last changes fastest.
Arguments:
- queries: bfloat16 [32768, 1024], P(('grp', 'seq')), may hold values from -6 to 6
- keys: bfloat16 [32768, 1024], P(('grp', 'seq')), may hold values from -11 to 11
- values: bfloat16 [32768, 1024], P(('grp', 'seq')), may hold values from -6 to 6
- forget: float32 [32768, 8], P(('grp', 'seq')), may hold values from 0 to 0.5
- beta: float32 [32768, 8], P(('grp', 'seq')), may hold values from 0 to 1
- level_weights: float32 [9, 32768, 8], P(None, ('grp', 'seq')), may hold values from 0.25 to 2
Outputs:
- output: float32 [32768, 1024], P(('grp', 'seq'))
The draws below stay inside these ranges and needn't reach their ends.
All inputs are finite; a program needn't handle non-finite values.
Results may differ from the reference program's by a relative error of at most 0.0003.
Values sent between devices are 32-bit elements; how exact they have to be, the bound alone decides.
No kernel may reach another device: no remote copies, remote signals or barrier semaphores. Data moves between devices by JAX's collectives and lax.ppermute only.
A program may use at most 64 MiB of HBM per device.

```python
import math
import jax
import jax.numpy as jnp
from jax import lax

HEADS = 8
HEAD_DIM = 128
BLOCK = 128
LEVELS = 8
TOK_DEV = 128
TOKENS = 32768
N_GRP = 4
N_SEQ = 64


def slow_heads(key):
    order = jax.random.permutation(jax.random.fold_in(key, 11), HEADS)
    count = HEADS // 2
    return order < count


def device_factor(key, salt):
    factor = jax.random.uniform(jax.random.fold_in(key, salt), (TOKENS // TOK_DEV, HEADS), jnp.float32, 0.6, 1.6)
    return jnp.repeat(factor, TOK_DEV, axis=0)


def draw_keys(key, part):
    subkeys = jax.random.split(jax.random.fold_in(key, 41), 3)
    noise_part = jnp.clip(jax.random.normal(subkeys[0], (TOKENS, HEADS, HEAD_DIM), jnp.float32), -6.0, 6.0)
    sign_pattern = (jax.random.randint(subkeys[1], (HEADS, HEAD_DIM), 0, 2) * 2 - 1).astype(jnp.float32)
    shared_scale = jax.random.uniform(subkeys[2], (TOKENS, HEADS), jnp.float32, 2.4, 3.6)
    result = noise_part + shared_scale[:, :, None] * sign_pattern[None, :, :]
    return result.reshape(TOKENS, HEADS * HEAD_DIM).astype(jnp.bfloat16)


def draw_forget(key, part):
    slow = slow_heads(key)
    subkeys = jax.random.split(jax.random.fold_in(key, 21), 6)
    slow_rate = jax.random.uniform(subkeys[0], (HEADS,), jnp.float32, 0.1, 0.5) / TOKENS
    fast_rate = jax.random.uniform(subkeys[1], (HEADS,), jnp.float32, 1.0 / 500.0, 1.0 / 250.0)
    base_rate = jnp.where(slow, slow_rate, fast_rate)
    rough = jax.random.uniform(subkeys[2], (TOKENS, HEADS), jnp.float32, 0.5, 1.5)
    result = base_rate[None, :] * device_factor(key, 23) * rough
    first_spot = jax.random.randint(subkeys[3], (HEADS,), 0, TOKENS)
    offset = jax.random.randint(subkeys[5], (HEADS,), 1, TOKENS)
    second_spot = (first_spot + offset) % TOKENS
    spots = jnp.stack([first_spot, second_spot], 0)
    amount = jax.random.uniform(subkeys[4], (2, HEADS), jnp.float32, 0.22, 0.4)
    columns = jnp.broadcast_to(jnp.arange(HEADS)[None, :], (2, HEADS))
    return result.at[spots, columns].add(amount)


def draw_beta(key, part):
    slow = slow_heads(key)
    subkeys = jax.random.split(jax.random.fold_in(key, 31), 3)
    slow_base = jax.random.uniform(subkeys[0], (HEADS,), jnp.float32, 0.5, 1.5) * 3.0 * HEAD_DIM / TOKENS
    fast_base = jax.random.uniform(subkeys[1], (HEADS,), jnp.float32, 0.2, 0.7)
    base_value = jnp.where(slow, slow_base, fast_base)
    rough = jax.random.uniform(subkeys[2], (TOKENS, HEADS), jnp.float32, 0.7, 1.3)
    return base_value[None, :] * rough


def block_scale(own_key, dims, shards, least, high):
    def one(dim, blocks):
        heights = jax.random.uniform(jax.random.fold_in(jax.random.fold_in(own_key, 6), dim), (blocks,), jnp.float32, least / len(shards), high / len(shards))
        return jnp.repeat(jnp.exp(heights), dims[dim] // blocks).reshape((-1,) + (1,) * (len(dims) - dim - 1))

    factor_of = one(*shards[0])
    for cut in shards[1:]:
        factor_of = factor_of * one(*cut)
    return factor_of


def centred(key, shape, spread, reach, cuts=(), held_as=jnp.bfloat16):
    gain = block_scale(key, shape, cuts, -0.22, 0.18) if cuts else 1.0
    values = jax.random.normal(key, shape, jnp.float32) * spread * gain
    return jnp.minimum(jnp.maximum(values, -reach), reach).astype(held_as)


def setup_inputs(seed: int = 0) -> dict:
    splits = jax.random.split(jax.random.key(seed), 7)
    queries = centred(splits[0], (TOKENS, HEADS * HEAD_DIM), 1.0, 6.0, ((0, 256),))
    keys = draw_keys(jax.random.fold_in(splits[6], 71), 0)
    values = centred(splits[2], (TOKENS, HEADS * HEAD_DIM), 1.0, 6.0, ((0, 256),))
    forget = draw_forget(jax.random.fold_in(splits[6], 71), 0)
    beta = draw_beta(jax.random.fold_in(splits[6], 71), 0)
    level_weights = jnp.clip(jnp.exp(math.log(2.0) - 2.0794415 * jax.random.uniform(splits[5], (LEVELS + 1, TOKENS, HEADS), jnp.float32) ** block_scale(splits[5], (LEVELS + 1, TOKENS, HEADS), ((1, 256),), -0.2, 0.2)), 0.25, 2.0)
    return {"queries": queries, "keys": keys, "values": values, "forget": forget, "beta": beta, "level_weights": level_weights}


def contract(form, left, right):
    return jnp.einsum(form, left, right, precision=lax.Precision.HIGHEST)

def unit_rows(array):
    return array * lax.rsqrt(lax.optimization_barrier(jnp.sum(array * array, -1, keepdims=True)) + 1e-06)

def block_step(carry, pieces):
    memory, transition = carry
    query_block, key_block, value_block, forget_block, beta_block = pieces
    length = query_block.shape[0]
    head_dim = query_block.shape[-1]
    query_heads = unit_rows(jnp.swapaxes(query_block.astype(jnp.float32), 0, 1))
    key_heads = unit_rows(jnp.swapaxes(key_block.astype(jnp.float32), 0, 1))
    value_heads = jnp.swapaxes(value_block.astype(jnp.float32), 0, 1)
    decays = jnp.exp(-jnp.cumsum(forget_block, 0)).T
    strength = beta_block.T
    strict = jnp.tril(jnp.ones((length, length), jnp.float32), -1)
    causal = jnp.tril(jnp.ones((length, length), jnp.float32), 0)
    intersections = contract('hsk,htk->hst', key_heads, key_heads)
    unit_lower = jnp.eye(length, dtype=jnp.float32) + strength[:, :, None] * intersections * strict
    right_sides = jnp.concatenate([strength[:, :, None] * key_heads, (strength / decays)[:, :, None] * value_heads], -1)
    solved = lax.linalg.triangular_solve(unit_lower, right_sides, left_side=True, lower=True, unit_diagonal=True)
    update_rows = solved[..., :head_dim]
    write_rows = solved[..., head_dim:]
    scores = contract('htk,hsk->hts', query_heads, key_heads) * causal
    reached = decays[:, :, None] * (query_heads - contract('hts,hsk->htk', scores, update_rows))
    inside = decays[:, :, None] * contract('hts,hsv->htv', scores, write_rows) + contract('hvk,htk->htv', memory, reached)
    reach_dev = contract('hkj,htj->htk', transition, reached)
    final_decay = decays[:, -1][:, None, None]
    step_trans = final_decay * (jnp.eye(head_dim, dtype=jnp.float32) - contract('hsk,hsj->hkj', update_rows, key_heads))
    step_write = final_decay * contract('hsv,hsk->hvk', write_rows, key_heads)
    memory = contract('hvk,hkj->hvj', memory, step_trans) + step_write
    transition = contract('hik,hkj->hij', transition, step_trans)
    return ((memory, transition), (inside, reach_dev))

def reference(queries, keys, values, forget, beta, level_weights):
    devices = N_GRP * N_SEQ
    blocks = TOK_DEV // BLOCK

    def per_device(array):
        return array.reshape((devices, blocks, BLOCK) + array.shape[1:])
    shaped = (TOKENS, HEADS, HEAD_DIM)
    weights_dev = jnp.transpose(level_weights, (1, 0, 2)).reshape(devices, TOK_DEV, LEVELS + 1, HEADS)
    items = (per_device(queries.reshape(shaped)), per_device(keys.reshape(shaped)), per_device(values.reshape(shaped)), per_device(forget), per_device(beta), weights_dev, jnp.arange(devices, dtype=jnp.int32))
    spans = jnp.left_shift(jnp.int32(1), jnp.arange(LEVELS, dtype=jnp.int32))

    def device_step(levels, entry):
        query_dev, key_dev, value_dev, forget_dev, beta_dev, weight_dev, number = entry
        start = (jnp.zeros((HEADS, HEAD_DIM, HEAD_DIM), jnp.float32), jnp.broadcast_to(jnp.eye(HEAD_DIM, dtype=jnp.float32), (HEADS, HEAD_DIM, HEAD_DIM)))
        (memory, transition), (inside, reached) = lax.scan(block_step, start, (query_dev, key_dev, value_dev, forget_dev, beta_dev))
        inside = jnp.swapaxes(inside, 0, 1).reshape(HEADS, TOK_DEV, HEAD_DIM)
        reached = jnp.swapaxes(reached, 0, 1).reshape(HEADS, TOK_DEV, HEAD_DIM)
        weighted = jnp.transpose(weight_dev[:, 1:, :], (1, 2, 0))[:, :, :, None] * reached[None]
        far_part = contract('lhtk,lhvk->htv', weighted, levels)
        result = weight_dev[:, 0, :].T[:, :, None] * inside + far_part
        following = number + 1
        below = following % (2 * spans) == 0
        target = jnp.logical_and(following % spans == 0, jnp.logical_not(below))
        moved = contract('lhvk,hkj->lhvj', levels, transition)
        merged = contract('lhvk,hkj->hvj', levels * below.astype(jnp.float32)[:, None, None, None], transition) + memory
        cleared = jnp.logical_or(below, target)[:, None, None, None]
        levels = jnp.where(cleared, jnp.zeros_like(moved), moved) + target.astype(jnp.float32)[:, None, None, None] * merged[None]
        return (levels, result)
    zeros = jnp.zeros((LEVELS, HEADS, HEAD_DIM, HEAD_DIM), jnp.float32)
    unused, results = lax.scan(device_step, zeros, items)
    return jnp.transpose(results, (0, 2, 1, 3)).reshape(TOKENS, HEADS * HEAD_DIM)
```

```python
import jax
import jax.numpy as jnp
from jax import lax
from jax.experimental import pallas as pl
from jax.experimental.pallas import tpu as pltpu
from jax.sharding import PartitionSpec as P

AXES = ("grp", "seq")
NY, NX, NZ, NC = 4, 4, 8, 2
HEADS = 8
D = 128
LEVELS = 8
F32 = jnp.float32
SQ = (D, D)
WIDE = (D, 2 * D)


BF16 = jnp.bfloat16


def halves(array):
    high = array.astype(BF16)
    return high, (array - high.astype(F32)).astype(BF16)


def mm_halves(left, right):
    n = right[0].shape[1]
    right = jnp.concatenate(right, 1)
    prod = jnp.dot(
        jnp.concatenate(left, 1),
        jnp.concatenate([right, right], 0),
        preferred_element_type=F32,
    )
    return prod[:, :n] + prod[:, n:]


def mm(left, right):
    return mm_halves(halves(left), halves(right))


def iotas(rows, cols):
    return (
        lax.broadcasted_iota(jnp.int32, (rows, cols), 0),
        lax.broadcasted_iota(jnp.int32, (rows, cols), 1),
    )


def unit_rows(array):
    return array * lax.rsqrt(jnp.sum(array * array, -1, keepdims=True) + 1e-06)


def place():
    seq = lax.axis_index("seq")
    return seq & 1, (seq >> 4) & 3, (seq >> 1) & 7, lax.axis_index("grp")


def head_span(h):
    return slice(h * D, (h + 1) * D)


def join(upper, lower):
    prod = mm(upper[:, :D], lower)
    return jnp.concatenate([prod[:, :D], prod[:, D:] + upper[:, D:]], 1)


def state_kernel(
    k_hbm, v_hbm, f_hbm, b_hbm, ab_ref, uw_ref, kt_ref, decay_ref,
    k_ref, v_ref, f_ref, b_ref, sems,
):
    copies = [
        pltpu.make_async_copy(source, target, sems.at[i])
        for i, (source, target) in enumerate(
            ((f_hbm, f_ref), (b_hbm, b_ref), (k_hbm, k_ref), (v_hbm, v_ref))
        )
    ]
    for copy in copies:
        copy.start()
    row, col = iotas(D, D)
    copies[0].wait()
    copies[1].wait()
    causal = row >= col
    eye = (row == col).astype(F32)
    total = jnp.dot(
        causal.astype(F32), f_ref[...].T,
        precision=lax.Precision.HIGHEST, preferred_element_type=F32,
    )
    decays = jnp.exp(-total)
    decay_ref[...] = decays
    strength = b_ref[...].T
    scaled = strength / decays
    heads = range(HEADS)
    copies[2].wait()
    ks = [unit_rows(k_ref[:, head_span(h)].astype(F32)) for h in heads]
    kts = [ks[h].T for h in heads]
    lowers = []
    for h in heads:
        kt_ref[h] = kts[h]
        cross = mm(ks[h], kts[h])
        lowers.append(jnp.where(row > col, cross * strength[:, h : h + 1], 0.0))

    def mask(j):
        same = (row >> (j + 1)) == (col >> (j + 1))
        return same & (((row >> j) & 1) == 1) & (((col >> j) & 1) == 0)

    inverse = [eye - jnp.where(mask(0), lowers[h], 0.0) for h in heads]
    parts = [halves(lowers[h]) for h in heads]
    for j in range(1, 7):
        pick = mask(j).astype(F32).astype(BF16)
        now = [halves(inverse[h]) for h in heads]
        half = [mm_halves(now[h], [part * pick for part in parts[h]]) for h in heads]
        inverse = [inverse[h] - mm_halves(halves(half[h]), now[h]) for h in heads]
    uws = []
    copies[3].wait()
    for h in heads:
        vh = v_ref[:, head_span(h)].astype(F32)
        right = jnp.concatenate(
            [strength[:, h : h + 1] * ks[h], scaled[:, h : h + 1] * vh], 1
        )
        uws.append(mm(inverse[h], right))
    for h in heads:
        uw_ref[h] = uws[h]
        final = decays[D - 1 : D, h : h + 1]
        prod = mm(kts[h], uws[h])
        ab_ref[h, :, :D] = final * (eye - prod[:, :D])
        ab_ref[h, :, D:] = final * prod[:, D:]


def read_kernel(q_ref, kt_ref, uw_ref, decay_ref, lw_ref, r_ref, in_ref):
    row, col = iotas(D, D)
    causal = row >= col
    decays = decay_ref[...]
    weights = lw_ref[0].T
    heads = range(HEADS)
    qs = [unit_rows(q_ref[:, head_span(h)].astype(F32)) for h in heads]
    scores = [jnp.where(causal, mm(qs[h], kt_ref[h]), 0.0) for h in heads]
    for h in heads:
        seen = mm(scores[h], uw_ref[h])
        decay = decays[:, h : h + 1]
        r_ref[h] = decay * (qs[h] - seen[:, :D])
        in_ref[:, head_span(h)] = decay * seen[:, D:] * weights[:, h : h + 1]


def pair_kernel(own_ref, peer_ref, x0_ref, x1_ref, x2_ref, x3_ref, x4_ref):
    core, _, z, _ = place()

    def emit(lower, upper, sign):
        for d, out in ((1, x1_ref), (2, x2_ref), (3, x3_ref)):
            h = (z + NZ + sign * d) & (NZ - 1)
            out[...] = join(upper[h], lower[h])
        h = (z + 4) & (NZ - 1)
        if sign > 0:
            x4_ref[...] = mm(upper[h][:, :D], lower[h][:, :D])
        else:
            x4_ref[...] = mm(upper[h][:, :D], lower[h][:, D:]) + upper[h][:, D:]
        x0_ref[...] = join(upper[z], lower[z])

    @pl.when(core == 0)
    def _():
        emit(own_ref, peer_ref, 1)

    @pl.when(core == 1)
    def _():
        emit(peer_ref, own_ref, -1)


def rows_kernel(peer_ref, r_ref, in_ref, lw_ref, rp_ref, acc_ref):
    core = place()[0]
    for level in range(1, LEVELS + 1):
        rp_ref[:, D + level - 1, :] = lw_ref[level]

    @pl.when(core == 0)
    def _():
        rp_ref[:, :D, :] = r_ref[...]
        acc_ref[...] = in_ref[...]

    @pl.when(core == 1)
    def _():
        weights = lw_ref[1].T
        for h in range(HEADS):
            moved = mm(r_ref[h], peer_ref[h])
            rp_ref[h, :D, :] = moved[:, :D]
            acc_ref[:, head_span(h)] = (
                in_ref[:, head_span(h)] + moved[:, D:] * weights[:, h : h + 1]
            )


def ring_kernel(
    x0_ref, y1_ref, y2_ref, y3_ref, y4_ref, p1_ref, p2_ref, p3_ref, p4_ref,
    even_ref, two_ref, four_ref, ab_ref, half_ref, one_ref,
):
    core, _, z, _ = place()
    back = lambda d: (z + NZ - d) & (NZ - 1)
    ahead = lambda d: (z + d) & (NZ - 1)
    one_ref[z] = x0_ref[...]
    across = ahead(4)

    @pl.when(core == 0)
    def _():
        for d, own, peer in ((1, y1_ref, p1_ref), (2, y2_ref, p2_ref), (3, y3_ref, p3_ref)):
            one_ref[back(d)] = own[...]
            one_ref[ahead(d)] = peer[...]
        one_ref[across, :, :D] = y4_ref[...]
        one_ref[across, :, D:] = p4_ref[...]

    @pl.when(core == 1)
    def _():
        for d, own, peer in ((1, y1_ref, p1_ref), (2, y2_ref, p2_ref), (3, y3_ref, p3_ref)):
            one_ref[ahead(d)] = own[...]
            one_ref[back(d)] = peer[...]
        one_ref[across, :, :D] = p4_ref[...]
        one_ref[across, :, D:] = y4_ref[...]

    two = [join(one_ref[c + 1], one_ref[c]) for c in range(0, NZ, 2)]
    for c in range(4):
        even_ref[c] = one_ref[2 * c]
    for c in range(2):
        two_ref[c] = two[2 * c]
    four = [join(two[c + 1], two[c]) for c in (0, 2)]
    four_ref[...] = four[0]
    whole = join(four[1], four[0])
    ab_ref[...] = whole
    half_ref[...] = jnp.where(core == 0, whole[:, :D], whole[:, D:])


def gather_runs(core, slot, own_ref, y1_ref, y2_ref, p1_ref, p2_ref, runs_ref):
    runs_ref[slot] = own_ref[...]
    back, ahead, across = (slot + 3) & 3, (slot + 1) & 3, (slot + 2) & 3

    @pl.when(core == 0)
    def _():
        runs_ref[back] = y1_ref[...]
        runs_ref[ahead] = p1_ref[...]
        runs_ref[across, :, :D] = y2_ref[...]
        runs_ref[across, :, D:] = p2_ref[...]

    @pl.when(core == 1)
    def _():
        runs_ref[ahead] = y1_ref[...]
        runs_ref[back] = p1_ref[...]
        runs_ref[across, :, :D] = p2_ref[...]
        runs_ref[across, :, D:] = y2_ref[...]


def x_kernel(
    own_ref, y1_ref, y2_ref, p1_ref, p2_ref,
    ab_ref, half_ref, prior_ref, g_ref, runs_ref,
):
    core, slot, _, _ = place()
    gather_runs(core, slot, own_ref, y1_ref, y2_ref, p1_ref, p2_ref, runs_ref)
    r0, r1, r2, r3 = (runs_ref[i] for i in range(4))
    low, high = join(r1, r0), join(r3, r2)
    whole = join(high, low)
    ab_ref[...] = whole
    half_ref[...] = jnp.where(core == 0, whole[:, :D], whole[:, D:])
    three = mm(r2[:, :D], low)
    row, col = iotas(D, D)
    eye = (row == col).astype(F32)
    zero = jnp.zeros(SQ, F32)
    prior = jnp.where(slot == 0, eye, r0[:, :D])
    prior = jnp.where(slot == 2, low[:, :D], prior)
    prior_ref[...] = jnp.where(slot == 3, three[:, :D], prior)
    g_ref[:, :D] = jnp.where(slot == 1, r0[:, D:], jnp.where(slot == 3, r2[:, D:], zero))
    g_ref[:, D:] = jnp.where(
        slot == 2, low[:, D:], jnp.where(slot == 3, three[:, D:], zero)
    )


def near_kernel(rp_ref, even_ref, two_ref, four_ref, g_ref, far_ref, moved_ref):
    third = mm(even_ref[1][:, :D], two_ref[0])
    seventh = mm(even_ref[3][:, :D], two_ref[1])
    fifth = mm(even_ref[2][:, :D], four_ref[...])
    sixth = mm(two_ref[1][:, :D], four_ref[...])
    last = mm(seventh[:, :D], four_ref[...])
    first = even_ref[0]
    quarter = two_ref[0]
    middle = four_ref[...]
    plans = [
        (None, []),
        (first[:, :D], [(1, first[:, D:])]),
        (quarter[:, :D], [(2, quarter[:, D:])]),
        (third[:, :D], [(1, even_ref[1][:, D:]), (2, third[:, D:])]),
        (middle[:, :D], [(3, middle[:, D:])]),
        (fifth[:, :D], [(1, even_ref[2][:, D:]), (3, fifth[:, D:])]),
        (sixth[:, :D], [(2, two_ref[1][:, D:]), (3, sixth[:, D:])]),
        (last[:, :D], [(1, even_ref[3][:, D:]), (2, seventh[:, D:]), (3, last[:, D:])]),
    ]
    moved, partial = [], []
    for c, (prior, levels) in enumerate(plans):
        rows = rp_ref[c, :D, :]
        weights = rp_ref[c, D:, :].T
        total = jnp.zeros(SQ, F32)
        if prior is None:
            moved.append(rows)
        else:
            prod = mm(rows, jnp.concatenate([prior] + [m for _, m in levels], 1))
            moved.append(prod[:, :D])
            for i, (level, _) in enumerate(levels):
                total = total + weights[:, level : level + 1] * prod[:, (i + 1) * D : (i + 2) * D]
        partial.append((total, weights))
    for c in range(NZ):
        total, weights = partial[c]
        prod = mm(moved[c], g_ref[...])
        far_ref[c] = total + weights[:, 4:5] * prod[:, :D] + weights[:, 5:6] * prod[:, D:]
        moved_ref[c, :, :D] = weights[:, 6:7] * moved[c]
        moved_ref[c, :, D:] = weights[:, 7:8] * moved[c]


def far_kernel(
    own_ref, y1_ref, y2_ref, p1_ref, p2_ref, prior_ref, near_ref, moved_ref,
    out_ref, runs_ref,
):
    core, _, _, slot = place()
    gather_runs(core, slot, own_ref, y1_ref, y2_ref, p1_ref, p2_ref, runs_ref)
    r0, r1, r2 = (runs_ref[i] for i in range(3))
    zero = jnp.zeros(SQ, F32)
    low = mm(r1[:, :D], r0[:, D:]) + r1[:, D:]
    three = mm(r2[:, :D], low)
    even = jnp.where(slot == 1, r0[:, D:], jnp.where(slot == 3, r2[:, D:], zero))
    pair = jnp.where(slot == 2, low, jnp.where(slot == 3, three, zero))
    mats = mm(prior_ref[...], jnp.concatenate([even, pair], 1))
    mats = jnp.concatenate([mats[:, :D], mats[:, D:]], 0)
    for c in range(NZ):
        out_ref[c] = near_ref[c] + mm(moved_ref[c], mats)


def add_kernel(acc_ref, far_ref, out_ref):
    for h in range(HEADS):
        out_ref[:, head_span(h)] = acc_ref[:, head_span(h)] + far_ref[h]


VMEM = pl.BlockSpec(memory_space=pltpu.VMEM)
HBM = pl.BlockSpec(memory_space=pltpu.HBM)


def call(kernel, outs, *args, scratch=(), products=1, space=VMEM, grant=16):
    sizes = [a.size * a.dtype.itemsize for a in args]
    return pl.pallas_call(
        kernel,
        out_shape=tuple(jax.ShapeDtypeStruct(s, F32) for s in outs),
        in_specs=[space] * len(args),
        out_specs=tuple(VMEM for _ in outs),
        scratch_shapes=scratch,
        cost_estimate=pl.CostEstimate(
            flops=products * 6 * D**3, bytes_accessed=sum(sizes), transcendentals=0
        ),
        compiler_params=pltpu.CompilerParams(vmem_limit_bytes=grant << 20),
    )(*args)


def send(block, move):
    pairs = []
    for i in range(NY * NX * NZ * NC):
        y, x, z, c = move(i >> 6, (i >> 4) & 3, (i >> 1) & 7, i & 1)
        pairs.append((i, ((y & 3) << 6) | ((x & 3) << 4) | ((z & 7) << 1) | c))
    return lax.ppermute(block, AXES, pairs)


def swap_core(block):
    return send(block, lambda y, x, z, c: (y, x, z, c ^ 1))


def over_z(block):
    groups = [
        [(x << 4) | (z << 1) | c for z in range(NZ)] for x in range(NX) for c in range(NC)
    ]
    return lax.all_to_all(block, "seq", 0, 0, axis_index_groups=groups, tiled=True)


def z_apart(block, d):
    return send(block, lambda y, x, z, c: (y, x, z + (d if c == 0 else -d), c))


def x_apart(block, d):
    return send(block, lambda y, x, z, c: (y, x + (d if c == 0 else -d), z, c))


def y_apart(block, d):
    return send(block, lambda y, x, z, c: (y + (d if c == 0 else -d), x, z, c))


def on_device(queries, keys, values, forget, beta, level_weights):
    weights = jnp.transpose(level_weights, (0, 2, 1))
    each = lambda n, shape: (n,) + shape
    ab, uw, kt, decays = call(
        state_kernel,
        [each(HEADS, WIDE), each(HEADS, WIDE), each(HEADS, SQ), (D, HEADS)],
        *(pltpu.with_memory_space_constraint(a, pltpu.HBM) for a in (keys, values, forget.T, beta.T)),
        products=150, space=HBM,
        scratch=[
            pltpu.VMEM((D, HEADS * D), jnp.bfloat16),
            pltpu.VMEM((D, HEADS * D), jnp.bfloat16),
            pltpu.VMEM((HEADS, D), F32),
            pltpu.VMEM((HEADS, D), F32),
            pltpu.SemaphoreType.DMA((4,)),
        ],
    )
    peer = swap_core(ab)
    reached, inside = call(
        read_kernel, [each(HEADS, SQ), (D, HEADS * D)],
        queries, kt, uw, decays, weights, products=24,
    )
    peer, reached, inside = lax.optimization_barrier((peer, reached, inside))
    x = call(
        pair_kernel, [WIDE, WIDE, WIDE, WIDE, SQ], ab, peer, products=9
    )
    y = [z_apart(x[d], d) for d in (4, 3, 2, 1)][::-1]
    rp, acc = call(
        rows_kernel, [(HEADS, D + LEVELS, D), (D, HEADS * D)],
        peer, reached, inside, weights, products=16,
    )
    *y, acc = lax.optimization_barrier((*y, acc))
    p = [swap_core(block) for block in y]
    one, two, four, ring, half = call(
        ring_kernel, [each(4, WIDE), each(2, WIDE), WIDE, WIDE, SQ],
        x[0], *y, *p, products=350, scratch=[pltpu.VMEM((NZ, D, 2 * D), F32)],
    )
    y1, y2 = x_apart(ring, 1), x_apart(half, 2)
    rows = over_z(rp)
    p1, p2 = swap_core(y1), swap_core(y2)
    runs = [pltpu.VMEM((4, D, 2 * D), F32)]
    plane, half, prior, gx = call(
        x_kernel, [WIDE, SQ, SQ, WIDE],
        ring, y1, y2, p1, p2, scratch=runs, products=8,
    )
    y1, y2 = y_apart(plane, 1), y_apart(half, 2)
    near, moved = call(
        near_kernel, [each(NZ, SQ), each(NZ, WIDE)], rows, one, two, four, gx, products=40
    )
    y2, near, moved = lax.optimization_barrier((y2, near, moved))
    p1, p2 = swap_core(y1), swap_core(y2)
    (far,) = call(
        far_kernel, [each(NZ, SQ)],
        plane, y1, y2, p1, p2, prior, near, moved,
        scratch=runs, products=20,
    )
    back = over_z(far)
    (out,) = call(add_kernel, [(D, HEADS * D)], acc, back)
    return out


def solution(mesh):
    spec = P(AXES, None)
    return jax.shard_map(
        on_device,
        mesh=mesh,
        in_specs=(spec, spec, spec, spec, spec, P(None, AXES, None)),
        out_specs=spec,
        check_vma=False,
    )
```

```python
import jax
import jax.numpy as jnp
from jax import lax
from jax.experimental import pallas as pl
from jax.experimental.pallas import tpu as pltpu
from jax.sharding import PartitionSpec as P

AXES = ("grp", "seq")
NY, NX, NZ, NC = 4, 4, 8, 2
HEADS = 8
D = 128
LEVELS = 8
F32 = jnp.float32
SQ = (D, D)
WIDE = (D, 2 * D)


BF16 = jnp.bfloat16


def halves(array):
    high = array.astype(BF16)
    return high, (array - high.astype(F32)).astype(BF16)


def mm_halves(left, right):
    n = right[0].shape[1]
    right = jnp.concatenate(right, 1)
    prod = jnp.dot(
        jnp.concatenate(left, 1),
        jnp.concatenate([right, right], 0),
        preferred_element_type=F32,
    )
    return prod[:, :n] + prod[:, n:]


def mm(left, right):
    return mm_halves(halves(left), halves(right))


def iotas(rows, cols):
    return (
        lax.broadcasted_iota(jnp.int32, (rows, cols), 0),
        lax.broadcasted_iota(jnp.int32, (rows, cols), 1),
    )


def unit_rows(array):
    return array * lax.rsqrt(jnp.sum(array * array, -1, keepdims=True) + 1e-06)


def place():
    seq = lax.axis_index("seq")
    return seq & 1, (seq >> 4) & 3, (seq >> 1) & 7, lax.axis_index("grp")


def head_span(h):
    return slice(h * D, (h + 1) * D)


def join(upper, lower):
    prod = mm(upper[:, :D], lower)
    return jnp.concatenate([prod[:, :D], prod[:, D:] + upper[:, D:]], 1)


def state_kernel(
    k_hbm, v_hbm, f_hbm, b_hbm, ab_ref, uw_ref, kt_ref, decay_ref,
    k_ref, v_ref, f_ref, b_ref, sems,
):
    copies = [
        pltpu.make_async_copy(source, target, sems.at[i])
        for i, (source, target) in enumerate(
            ((f_hbm, f_ref), (b_hbm, b_ref), (k_hbm, k_ref), (v_hbm, v_ref))
        )
    ]
    for copy in copies:
        copy.start()
    row, col = iotas(D, D)
    copies[0].wait()
    copies[1].wait()
    causal = row >= col
    eye = (row == col).astype(F32)
    total = jnp.dot(
        causal.astype(F32), f_ref[...].T,
        precision=lax.Precision.HIGHEST, preferred_element_type=F32,
    )
    decays = jnp.exp(-total)
    decay_ref[...] = decays
    strength = b_ref[...].T
    scaled = strength / decays
    heads = range(HEADS)
    copies[2].wait()
    ks = [unit_rows(k_ref[:, head_span(h)].astype(F32)) for h in heads]
    kts = [ks[h].T for h in heads]
    lowers = []
    for h in heads:
        kt_ref[h] = kts[h]
        cross = mm(ks[h], kts[h])
        lowers.append(jnp.where(row > col, cross * strength[:, h : h + 1], 0.0))

    def mask(j):
        same = (row >> (j + 1)) == (col >> (j + 1))
        return same & (((row >> j) & 1) == 1) & (((col >> j) & 1) == 0)

    inverse = [eye - jnp.where(mask(0), lowers[h], 0.0) for h in heads]
    parts = [halves(lowers[h]) for h in heads]
    for j in range(1, 7):
        pick = mask(j).astype(F32).astype(BF16)
        now = [halves(inverse[h]) for h in heads]
        half = [mm_halves(now[h], [part * pick for part in parts[h]]) for h in heads]
        inverse = [inverse[h] - mm_halves(halves(half[h]), now[h]) for h in heads]
    uws = []
    copies[3].wait()
    for h in heads:
        vh = v_ref[:, head_span(h)].astype(F32)
        right = jnp.concatenate(
            [strength[:, h : h + 1] * ks[h], scaled[:, h : h + 1] * vh], 1
        )
        uws.append(mm(inverse[h], right))
    for h in heads:
        uw_ref[h] = uws[h]
        final = decays[D - 1 : D, h : h + 1]
        prod = mm(kts[h], uws[h])
        ab_ref[h, :, :D] = final * (eye - prod[:, :D])
        ab_ref[h, :, D:] = final * prod[:, D:]


def read_kernel(q_ref, kt_ref, uw_ref, decay_ref, lw_ref, r_ref, in_ref):
    row, col = iotas(D, D)
    causal = row >= col
    decays = decay_ref[...]
    weights = lw_ref[0].T
    heads = range(HEADS)
    qs = [unit_rows(q_ref[:, head_span(h)].astype(F32)) for h in heads]
    scores = [jnp.where(causal, mm(qs[h], kt_ref[h]), 0.0) for h in heads]
    for h in heads:
        seen = mm(scores[h], uw_ref[h])
        decay = decays[:, h : h + 1]
        r_ref[h] = decay * (qs[h] - seen[:, :D])
        in_ref[:, head_span(h)] = decay * seen[:, D:] * weights[:, h : h + 1]


def pair_kernel(own_ref, peer_ref, x0_ref, x1_ref, x2_ref, x3_ref, x4_ref):
    core, _, z, _ = place()

    def emit(lower, upper, sign):
        for d, out in ((1, x1_ref), (2, x2_ref), (3, x3_ref)):
            h = (z + NZ + sign * d) & (NZ - 1)
            out[...] = join(upper[h], lower[h])
        h = (z + 4) & (NZ - 1)
        if sign > 0:
            x4_ref[...] = mm(upper[h][:, :D], lower[h][:, :D])
        else:
            x4_ref[...] = mm(upper[h][:, :D], lower[h][:, D:]) + upper[h][:, D:]
        x0_ref[...] = join(upper[z], lower[z])

    @pl.when(core == 0)
    def _():
        emit(own_ref, peer_ref, 1)

    @pl.when(core == 1)
    def _():
        emit(peer_ref, own_ref, -1)


def rows_kernel(peer_ref, r_ref, in_ref, lw_ref, rp_ref, acc_ref):
    core = place()[0]
    for level in range(1, LEVELS + 1):
        rp_ref[:, D + level - 1, :] = lw_ref[level]

    @pl.when(core == 0)
    def _():
        rp_ref[:, :D, :] = r_ref[...]
        acc_ref[...] = in_ref[...]

    @pl.when(core == 1)
    def _():
        weights = lw_ref[1].T
        for h in range(HEADS):
            moved = mm(r_ref[h], peer_ref[h])
            rp_ref[h, :D, :] = moved[:, :D]
            acc_ref[:, head_span(h)] = (
                in_ref[:, head_span(h)] + moved[:, D:] * weights[:, h : h + 1]
            )


def ring_kernel(
    x0_ref, y1_ref, y2_ref, y3_ref, y4_ref, p1_ref, p2_ref, p3_ref, p4_ref,
    even_ref, two_ref, four_ref, ab_ref, half_ref, one_ref,
):
    core, _, z, _ = place()
    back = lambda d: (z + NZ - d) & (NZ - 1)
    ahead = lambda d: (z + d) & (NZ - 1)
    one_ref[z] = x0_ref[...]
    across = ahead(4)

    @pl.when(core == 0)
    def _():
        for d, own, peer in ((1, y1_ref, p1_ref), (2, y2_ref, p2_ref), (3, y3_ref, p3_ref)):
            one_ref[back(d)] = own[...]
            one_ref[ahead(d)] = peer[...]
        one_ref[across, :, :D] = y4_ref[...]
        one_ref[across, :, D:] = p4_ref[...]

    @pl.when(core == 1)
    def _():
        for d, own, peer in ((1, y1_ref, p1_ref), (2, y2_ref, p2_ref), (3, y3_ref, p3_ref)):
            one_ref[ahead(d)] = own[...]
            one_ref[back(d)] = peer[...]
        one_ref[across, :, :D] = p4_ref[...]
        one_ref[across, :, D:] = y4_ref[...]

    two = [join(one_ref[c + 1], one_ref[c]) for c in range(0, NZ, 2)]
    for c in range(4):
        even_ref[c] = one_ref[2 * c]
    for c in range(2):
        two_ref[c] = two[2 * c]
    four = [join(two[c + 1], two[c]) for c in (0, 2)]
    four_ref[...] = four[0]
    whole = join(four[1], four[0])
    ab_ref[...] = whole
    half_ref[...] = jnp.where(core == 0, whole[:, :D], whole[:, D:])


def gather_runs(core, slot, own_ref, y1_ref, y2_ref, p1_ref, p2_ref, runs_ref):
    runs_ref[slot] = own_ref[...]
    back, ahead, across = (slot + 3) & 3, (slot + 1) & 3, (slot + 2) & 3

    @pl.when(core == 0)
    def _():
        runs_ref[back] = y1_ref[...]
        runs_ref[ahead] = p1_ref[...]
        runs_ref[across, :, :D] = y2_ref[...]
        runs_ref[across, :, D:] = p2_ref[...]

    @pl.when(core == 1)
    def _():
        runs_ref[ahead] = y1_ref[...]
        runs_ref[back] = p1_ref[...]
        runs_ref[across, :, :D] = p2_ref[...]
        runs_ref[across, :, D:] = y2_ref[...]


def x_kernel(
    own_ref, y1_ref, y2_ref, p1_ref, p2_ref,
    ab_ref, half_ref, prior_ref, g_ref, runs_ref,
):
    core, slot, _, _ = place()
    gather_runs(core, slot, own_ref, y1_ref, y2_ref, p1_ref, p2_ref, runs_ref)
    r0, r1, r2, r3 = (runs_ref[i] for i in range(4))
    low, high = join(r1, r0), join(r3, r2)
    whole = join(high, low)
    ab_ref[...] = whole
    half_ref[...] = jnp.where(core == 0, whole[:, :D], whole[:, D:])
    three = mm(r2[:, :D], low)
    row, col = iotas(D, D)
    eye = (row == col).astype(F32)
    zero = jnp.zeros(SQ, F32)
    prior = jnp.where(slot == 0, eye, r0[:, :D])
    prior = jnp.where(slot == 2, low[:, :D], prior)
    prior_ref[...] = jnp.where(slot == 3, three[:, :D], prior)
    g_ref[:, :D] = jnp.where(slot == 1, r0[:, D:], jnp.where(slot == 3, r2[:, D:], zero))
    g_ref[:, D:] = jnp.where(
        slot == 2, low[:, D:], jnp.where(slot == 3, three[:, D:], zero)
    )


def near_kernel(rp_ref, even_ref, two_ref, four_ref, g_ref, prior_ref, far_ref, moved_ref):
    third = mm(even_ref[1][:, :D], two_ref[0])
    seventh = mm(even_ref[3][:, :D], two_ref[1])
    fifth = mm(even_ref[2][:, :D], four_ref[...])
    sixth = mm(two_ref[1][:, :D], four_ref[...])
    last = mm(seventh[:, :D], four_ref[...])
    first = even_ref[0]
    quarter = two_ref[0]
    middle = four_ref[...]
    plans = [
        (None, []),
        (first[:, :D], [(1, first[:, D:])]),
        (quarter[:, :D], [(2, quarter[:, D:])]),
        (third[:, :D], [(1, even_ref[1][:, D:]), (2, third[:, D:])]),
        (middle[:, :D], [(3, middle[:, D:])]),
        (fifth[:, :D], [(1, even_ref[2][:, D:]), (3, fifth[:, D:])]),
        (sixth[:, :D], [(2, two_ref[1][:, D:]), (3, sixth[:, D:])]),
        (last[:, :D], [(1, even_ref[3][:, D:]), (2, seventh[:, D:]), (3, last[:, D:])]),
    ]
    moved, partial = [], []
    for c, (prior, levels) in enumerate(plans):
        rows = rp_ref[c, :D, :]
        weights = rp_ref[c, D:, :].T
        total = jnp.zeros(SQ, F32)
        if prior is None:
            moved.append(rows)
        else:
            prod = mm(rows, jnp.concatenate([prior] + [m for _, m in levels], 1))
            moved.append(prod[:, :D])
            for i, (level, _) in enumerate(levels):
                total = total + weights[:, level : level + 1] * prod[:, (i + 1) * D : (i + 2) * D]
        partial.append((total, weights))
    for c in range(NZ):
        total, weights = partial[c]
        prod = mm(moved[c], jnp.concatenate([g_ref[...], prior_ref[...]], 1))
        carried = prod[:, 2 * D :]
        far_ref[c] = total + weights[:, 4:5] * prod[:, :D] + weights[:, 5:6] * prod[:, D : 2 * D]
        moved_ref[c, :, :D] = weights[:, 6:7] * carried
        moved_ref[c, :, D:] = weights[:, 7:8] * carried


def far_kernel(
    own_ref, y1_ref, y2_ref, p1_ref, p2_ref, near_ref, moved_ref,
    out_ref, runs_ref,
):
    core, _, _, slot = place()
    gather_runs(core, slot, own_ref, y1_ref, y2_ref, p1_ref, p2_ref, runs_ref)
    r0, r1, r2 = (runs_ref[i] for i in range(3))
    zero = jnp.zeros(SQ, F32)
    low = mm(r1[:, :D], r0[:, D:]) + r1[:, D:]
    three = mm(r2[:, :D], low)
    even = jnp.where(slot == 1, r0[:, D:], jnp.where(slot == 3, r2[:, D:], zero))
    pair = jnp.where(slot == 2, low, jnp.where(slot == 3, three, zero))
    mats = jnp.concatenate([even, pair], 0)
    for c in range(NZ):
        out_ref[c] = near_ref[c] + mm(moved_ref[c], mats)


def add_kernel(acc_ref, far_ref, out_hbm, out_ref, sems):
    copies = []
    for i in range(4):
        rows = slice(32 * i, 32 * (i + 1))
        for h in range(HEADS):
            out_ref[rows, head_span(h)] = acc_ref[rows, head_span(h)] + far_ref[h, rows, :]
        copy = pltpu.make_async_copy(out_ref.at[rows], out_hbm.at[rows], sems.at[i])
        copy.start()
        copies.append(copy)
    for copy in copies:
        copy.wait()


VMEM = pl.BlockSpec(memory_space=pltpu.VMEM)
HBM = pl.BlockSpec(memory_space=pltpu.HBM)


def call(kernel, outs, *args, scratch=(), products=1, space=VMEM, out_space=VMEM, grant=16):
    sizes = [a.size * a.dtype.itemsize for a in args]
    return pl.pallas_call(
        kernel,
        out_shape=tuple(jax.ShapeDtypeStruct(s, F32) for s in outs),
        in_specs=[space] * len(args),
        out_specs=tuple(out_space for _ in outs),
        scratch_shapes=scratch,
        cost_estimate=pl.CostEstimate(
            flops=products * 6 * D**3, bytes_accessed=sum(sizes), transcendentals=0
        ),
        compiler_params=pltpu.CompilerParams(vmem_limit_bytes=grant << 20),
    )(*args)


def send(block, move):
    pairs = []
    for i in range(NY * NX * NZ * NC):
        y, x, z, c = move(i >> 6, (i >> 4) & 3, (i >> 1) & 7, i & 1)
        pairs.append((i, ((y & 3) << 6) | ((x & 3) << 4) | ((z & 7) << 1) | c))
    return lax.ppermute(block, AXES, pairs)


def swap_core(block):
    return send(block, lambda y, x, z, c: (y, x, z, c ^ 1))


def over_z(block):
    groups = [
        [(x << 4) | (z << 1) | c for z in range(NZ)] for x in range(NX) for c in range(NC)
    ]
    return lax.all_to_all(block, "seq", 0, 0, axis_index_groups=groups, tiled=True)


def z_apart(block, d):
    return send(block, lambda y, x, z, c: (y, x, z + (d if c == 0 else -d), c))


def x_apart(block, d):
    return send(block, lambda y, x, z, c: (y, x + (d if c == 0 else -d), z, c))


def y_apart(block, d):
    return send(block, lambda y, x, z, c: (y + (d if c == 0 else -d), x, z, c))


def on_device(queries, keys, values, forget, beta, level_weights):
    weights = jnp.transpose(level_weights, (0, 2, 1))
    each = lambda n, shape: (n,) + shape
    ab, uw, kt, decays = call(
        state_kernel,
        [each(HEADS, WIDE), each(HEADS, WIDE), each(HEADS, SQ), (D, HEADS)],
        *(pltpu.with_memory_space_constraint(a, pltpu.HBM) for a in (keys, values, forget.T, beta.T)),
        products=150, space=HBM,
        scratch=[
            pltpu.VMEM((D, HEADS * D), jnp.bfloat16),
            pltpu.VMEM((D, HEADS * D), jnp.bfloat16),
            pltpu.VMEM((HEADS, D), F32),
            pltpu.VMEM((HEADS, D), F32),
            pltpu.SemaphoreType.DMA((4,)),
        ],
    )
    peer = swap_core(ab)
    reached, inside = call(
        read_kernel, [each(HEADS, SQ), (D, HEADS * D)],
        queries, kt, uw, decays, weights, products=24,
    )
    peer, reached, inside = lax.optimization_barrier((peer, reached, inside))
    x = call(
        pair_kernel, [WIDE, WIDE, WIDE, WIDE, SQ], ab, peer, products=9
    )
    y = [z_apart(x[d], d) for d in (4, 3, 2, 1)][::-1]
    rp, acc = call(
        rows_kernel, [(HEADS, D + LEVELS, D), (D, HEADS * D)],
        peer, reached, inside, weights, products=16,
    )
    *y, acc = lax.optimization_barrier((*y, acc))
    p = [swap_core(block) for block in y]
    one, two, four, ring, half = call(
        ring_kernel, [each(4, WIDE), each(2, WIDE), WIDE, WIDE, SQ],
        x[0], *y, *p, products=350, scratch=[pltpu.VMEM((NZ, D, 2 * D), F32)],
    )
    y1, y2 = x_apart(ring, 1), x_apart(half, 2)
    rows = over_z(rp)
    p1, p2 = swap_core(y1), swap_core(y2)
    runs = [pltpu.VMEM((4, D, 2 * D), F32)]
    plane, half, prior, gx = call(
        x_kernel, [WIDE, SQ, SQ, WIDE],
        ring, y1, y2, p1, p2, scratch=runs, products=8,
    )
    y1, y2 = y_apart(plane, 1), y_apart(half, 2)
    near, moved = call(
        near_kernel, [each(NZ, SQ), each(NZ, WIDE)], rows, one, two, four, gx, prior, products=40
    )
    y2, near, moved = lax.optimization_barrier((y2, near, moved))
    p1, p2 = swap_core(y1), swap_core(y2)
    (far,) = call(
        far_kernel, [each(NZ, SQ)],
        plane, y1, y2, p1, p2, near, moved,
        scratch=runs, products=20,
    )
    back = over_z(far)
    (out,) = call(
        add_kernel, [(D, HEADS * D)], acc, back, out_space=HBM,
        scratch=[pltpu.VMEM((D, HEADS * D), F32), pltpu.SemaphoreType.DMA((4,))],
    )
    return out


def solution(mesh):
    spec = P(AXES, None)
    return jax.shard_map(
        on_device,
        mesh=mesh,
        in_specs=(spec, spec, spec, spec, spec, P(None, AXES, None)),
        out_specs=spec,
        check_vma=False,
    )
```
